256 devices in a mesh: tm: 16 (over z, x_lo), space: 16 (over x_hi, y, core).
Axes of the slice: x: 4 (x_hi: 2, x_lo: 2; x = x_hi * 2 + x_lo), y: 4, z: 8, core: 2. Of those that a mesh axis runs over, the one named last changes fastest.
Arguments:
- slice_starts: float32 [16, 64, 512, 128], P('tm', 'space'), may hold values from -6 to 6
- diffusion: float32 [64, 512, 128], P('space'), may hold values from 0.01 to 0.05
- courant: float32 [64, 512, 128], P('space'), may hold values from 0.3 to 0.6
- loss: float32 [64, 512, 128], P('space'), may hold values from 0.002 to 0.02
- heating: float32 [64, 512, 128], P('space'), may hold values from -0.6 to 0.6
Outputs:
- end_states: float32 [16, 64, 512, 128], P('tm', 'space')
- next_starts: float32 [16, 64, 512, 128], P('tm', 'space')
The draws below stay inside these ranges and needn't reach their ends.
All inputs are finite; a program needn't handle non-finite values.
Results may differ from the reference program's by a relative error of at most 0.00002.
Values sent between devices are 32-bit elements; how exact they have to be, the bound alone decides.
No kernel may reach another device: no remote copies, remote signals or barrier semaphores. Data moves between devices by JAX's collectives and lax.ppermute only.
A program may use at most 128 MiB of HBM per device.

```python
import math
import jax
import jax.numpy as jnp
from jax import lax

NY = 512
NZ = 128
FINE = 8
NX = 64
SLICES = 16
N_TM = 16


def block_levels(rng, extent, split, least, high):
    gain, own = 1.0, jax.random.fold_in(rng, 6)
    for position, shards_of in split:
        heights = jnp.exp(jax.random.uniform(jax.random.fold_in(own, position), (shards_of,), jnp.float32, least / len(split), high / len(split)))
        gain = gain * jnp.repeat(heights, extent[position] // shards_of).reshape([-1 if axis == position else 1 for axis in range(len(extent))])
    return gain


def bell_draw(stream_key, shape, spread, bound, split=(), kind=jnp.bfloat16):
    entries = spread * jax.random.normal(stream_key, shape, jnp.float32)
    if split:
        entries = entries * block_levels(stream_key, shape, split, -0.22, 0.18)
    return jnp.clip(entries, -bound, bound).astype(kind)


def setup_inputs(seed: int = 0) -> dict:
    seeds = jax.random.split(jax.random.key(seed), 6)
    slice_starts = bell_draw(seeds[0], (SLICES, NX, NY, NZ), 1.0, 6.0, ((0, 16), (1, 16)), jnp.float32)
    diffusion = jnp.clip(jnp.exp(math.log(0.05) - 1.609438 * jax.random.uniform(seeds[1], (NX, NY, NZ), jnp.float32) ** block_levels(seeds[1], (NX, NY, NZ), ((0, 16),), -0.2, 0.2)), 0.01, 0.05)
    courant = jnp.clip(0.3 + 0.3 * jax.random.uniform(seeds[2], (NX, NY, NZ), jnp.float32) ** block_levels(seeds[2], (NX, NY, NZ), ((0, 16),), -0.2, 0.2), 0.3, 0.6)
    loss = jnp.clip(jnp.exp(math.log(0.02) - 2.30258502 * jax.random.uniform(seeds[3], (NX, NY, NZ), jnp.float32) ** block_levels(seeds[3], (NX, NY, NZ), ((0, 16),), -0.2, 0.2)), 0.002, 0.02)
    heating = bell_draw(seeds[4], (NX, NY, NZ), 0.1, 0.6, ((0, 16),), jnp.float32)
    return dict(slice_starts=slice_starts, diffusion=diffusion, courant=courant, loss=loss, heating=heating)


def neighbours(v):
    padded = jnp.pad(v, 1)
    total = padded[2:, 1:-1, 1:-1] + padded[:-2, 1:-1, 1:-1]
    total = total + padded[1:-1, 2:, 1:-1] + padded[1:-1, :-2, 1:-1]
    total = total + padded[1:-1, 1:-1, 2:] + padded[1:-1, 1:-1, :-2]
    return total, padded[:-2, 1:-1, 1:-1]


def fine_step(v, diffusion, courant, loss, heating):
    total, upwind = neighbours(v)
    return v + diffusion * (total - 6.0 * v) - courant * (v - upwind) - loss * v + heating


def coarse(v, diffusion, courant, loss, heating):
    total, upwind = neighbours(v)
    denom = 1.0 + FINE * (6.0 * diffusion + courant + loss)
    return (v + FINE * (diffusion * total + courant * upwind + heating)) / denom


def reference(slice_starts, diffusion, courant, loss, heating):
    def propagate(start):
        state = start
        for step in range(FINE):
            state = fine_step(state, diffusion, courant, loss, heating)
        return state

    fine_ends = lax.map(propagate, slice_starts)
    coarse_old = lax.map(lambda v: coarse(v, diffusion, courant, loss, heating), slice_starts)
    current = slice_starts[0]
    ends = []
    for index in range(N_TM):
        current = coarse(current, diffusion, courant, loss, heating) + fine_ends[index] - coarse_old[index]
        ends.append(current)
    end_states = jnp.stack(ends)
    next_starts = jnp.concatenate([slice_starts[:1], end_states[:-1]], axis=0)
    return end_states, next_starts
```

```python
import jax
import jax.numpy as jnp
from jax import lax
from jax.sharding import PartitionSpec as P

FINE = 8
SPAN = 4
ROUNDS = 2


def swaps(pairs):
    return [route for a, b in pairs for route in ((a, b), (b, a))]


def exchanged(low, high, even):
    devices = lax.axis_size("space")
    near = swaps([(i, i + 1) for i in range(0, devices - 1, 2)])
    far = swaps([(i, i + 1) for i in range(1, devices - 1, 2)])
    across = lax.ppermute(jnp.where(even, low, high), "space", far)
    beside = lax.ppermute(jnp.where(even, high, low), "space", near)
    return jnp.where(even, across, beside), jnp.where(even, beside, across)


def around(wide):
    padded = jnp.pad(wide, ((0, 0), (1, 1), (1, 1)))
    total = padded[2:, 1:-1, 1:-1] + padded[:-2, 1:-1, 1:-1]
    total = total + padded[1:-1, 2:, 1:-1] + padded[1:-1, :-2, 1:-1]
    total = total + padded[1:-1, 1:-1, 2:] + padded[1:-1, 1:-1, :-2]
    return total, wide[:-2]


def on_device(slice_starts, diffusion, courant, loss, heating):
    start = slice_starts[0]
    planes, rows, lanes = start.shape
    slices = lax.axis_size("tm")
    slot = lax.axis_index("tm")
    even = lax.axis_index("space") % 2 == 0
    part = rows // slices
    halo = slices
    window = part + 2 * halo

    denom = 1.0 + FINE * (6.0 * diffusion + courant + loss)
    own = 1.0 / denom
    side = FINE * diffusion / denom
    west = FINE * courant / denom

    fine_terms = jnp.stack([diffusion, courant, loss, heating])
    tall = jnp.pad(jnp.stack([own, side, west]), ((0, 0), (0, 0), (halo, halo), (0, 0)))
    coarse_terms = lax.dynamic_slice_in_dim(tall, slot * part, window, axis=2)
    deep = SPAN - 1
    edge = ROUNDS - 1

    def flat(*arrays):
        return jnp.concatenate([a.reshape(-1, lanes) for a in arrays])

    before, after = exchanged(
        flat(fine_terms[:, :edge], coarse_terms[:, :deep]),
        flat(fine_terms[:, planes - edge :], coarse_terms[:, planes - deep :]),
        even,
    )
    cut = 4 * edge * rows

    def fine_part(x):
        return x[:cut].reshape(4, edge, rows, lanes)

    def coarse_part(x):
        return x[cut:].reshape(3, deep, window, lanes)

    fine_terms = jnp.concatenate([fine_part(before), fine_terms, fine_part(after)], axis=1)
    coarse_terms = jnp.concatenate([coarse_part(before), coarse_terms, coarse_part(after)], axis=1)

    state = start
    first = None
    for _ in range(FINE // ROUNDS):
        before, after = exchanged(state[:ROUNDS], state[planes - ROUNDS :], even)
        state = jnp.concatenate([before, state, after])
        if first is None:
            first = state[ROUNDS - 1 : ROUNDS + planes + 1]
        for step in range(ROUNDS):
            total, upwind = around(state)
            centre = state[1:-1]
            trim = step
            d, c, l, h = (t[trim : t.shape[0] - trim] for t in fine_terms)
            state = centre + d * (total - 6.0 * centre) - c * (centre - upwind) - l * centre + h
    total, upwind = around(first)
    coarse_old = own * start + side * total + west * upwind
    element = jnp.where(slot > 0, state - coarse_old, state)

    blocks = jnp.pad(element, ((0, 0), (halo, halo), (0, 0))).reshape(planes, -1, part, lanes)
    widened = jnp.concatenate([blocks[:, :-1], blocks[:, 1:]], axis=2)
    terms = lax.all_to_all(widened.transpose(1, 0, 2, 3), "tm", 0, 0, tiled=True)

    depth = [SPAN] + [(SPAN - n) % SPAN for n in range(1, slices)]
    before, after = exchanged(
        jnp.concatenate([terms[n, :k] for n, k in enumerate(depth) if k]),
        jnp.concatenate([terms[n, planes - k :] for n, k in enumerate(depth) if k]),
        even,
    )
    offsets = [sum(depth[:n]) for n in range(slices)]

    def term(n):
        k, o = depth[n], offsets[n]
        return jnp.concatenate([before[o : o + k], terms[n], after[o : o + k]]) if k else terms[n]

    state = term(0)
    ends = [terms[0]]
    for n in range(1, slices):
        if n > 1 and n % SPAN == 1:
            low, high = exchanged(state, state, even)
            state = jnp.concatenate([low, state, high])
        k = depth[n]
        trim = deep - k
        o, s, w = (t[trim : t.shape[0] - trim] for t in coarse_terms)
        total, upwind = around(state)
        state = o * state[1:-1] + s * total + w * upwind + term(n)
        ends.append(state[k : k + planes])

    ends = jnp.stack(ends)[:, :, halo : halo + part]
    back = lax.all_to_all(ends, "tm", 0, 0, tiled=True)
    end_state = back.transpose(1, 0, 2, 3).reshape(planes, rows, lanes)
    arrived = lax.ppermute(end_state, "tm", [(i, i + 1) for i in range(slices - 1)])
    following = jnp.where(slot == 0, start, arrived)
    return end_state[None], following[None]


def solution(mesh):
    return jax.shard_map(
        on_device,
        mesh=mesh,
        in_specs=(
            P("tm", "space", None, None),
            P("space", None, None),
            P("space", None, None),
            P("space", None, None),
            P("space", None, None),
        ),
        out_specs=(P("tm", "space", None, None), P("tm", "space", None, None)),
        check_vma=False,
    )
```

```python
import jax
import jax.numpy as jnp
from jax import lax
from jax.sharding import PartitionSpec as P

FINE = 8
SPAN = 4
ROUNDS = 2
STREAMS = 2


def swaps(pairs):
    return [route for a, b in pairs for route in ((a, b), (b, a))]


def exchanged(low, high, even):
    devices = lax.axis_size("space")
    near = swaps([(i, i + 1) for i in range(0, devices - 1, 2)])
    far = swaps([(i, i + 1) for i in range(1, devices - 1, 2)])
    across = lax.ppermute(jnp.where(even, low, high), "space", far)
    beside = lax.ppermute(jnp.where(even, high, low), "space", near)
    return jnp.where(even, across, beside), jnp.where(even, beside, across)


def around(wide):
    padded = jnp.pad(wide, ((0, 0), (1, 1), (1, 1)))
    total = padded[2:, 1:-1, 1:-1] + padded[:-2, 1:-1, 1:-1]
    total = total + padded[1:-1, 2:, 1:-1] + padded[1:-1, :-2, 1:-1]
    total = total + padded[1:-1, 1:-1, 2:] + padded[1:-1, 1:-1, :-2]
    return total, wide[:-2]


def on_device(slice_starts, diffusion, courant, loss, heating):
    start = slice_starts[0]
    planes, rows, lanes = start.shape
    slices = lax.axis_size("tm")
    slot = lax.axis_index("tm")
    even = lax.axis_index("space") % 2 == 0
    part = rows // slices
    halo = slices
    window = part + 2 * halo

    deep = SPAN - 1
    edge = ROUNDS - 1
    fine_terms = (diffusion, courant, loss, heating)

    def cut_window(x):
        tall = jnp.pad(x, ((0, 0), (halo, halo), (0, 0)))
        return lax.dynamic_slice_in_dim(tall, slot * part, window, axis=1)

    def flat(*arrays):
        return jnp.concatenate([a.reshape(-1, lanes) for a in arrays])

    coarse_terms = [cut_window(x) for x in fine_terms[:3]]
    half = rows // STREAMS
    bounds = [(max(0, i * half - FINE), min(rows, (i + 1) * half + FINE)) for i in range(STREAMS)]
    starts = [start[:, lo:hi] for lo, hi in bounds]

    def edges(x, width):
        return x[:width], x[x.shape[0] - width :]

    ends_of = [edges(x, edge) for x in fine_terms] + [edges(x, deep) for x in coarse_terms] + [edges(starts[0], ROUNDS)]
    before, after = exchanged(flat(*[x for x, _ in ends_of]), flat(*[x for _, x in ends_of]), even)

    def split(x):
        out, at = [], 0
        for piece, _ in ends_of:
            size = piece.shape[0] * piece.shape[1]
            out.append(x[at : at + size].reshape(piece.shape))
            at += size
        return out

    wide = [jnp.concatenate([lo, x, hi]) for lo, x, hi in zip(split(before), list(fine_terms) + coarse_terms + [starts[0]], split(after))]
    fine_wide, coarse_wide, firsts = wide[:4], wide[4:7], [wide[7]]
    for x in starts[1:]:
        before, after = exchanged(*edges(x, ROUNDS), even)
        firsts.append(jnp.concatenate([before, x, after]))

    def coarse_factors(d, c, l, inside=1.0):
        denom = 1.0 + FINE * (6.0 * d + c + l)
        return inside / denom, FINE * d / denom, FINE * c / denom

    states = list(firsts)
    for turn in range(FINE // ROUNDS):
        for i, (lo, hi) in enumerate(bounds):
            state = states[i]
            if turn:
                before, after = exchanged(*edges(state, ROUNDS), even)
                state = jnp.concatenate([before, state, after])
            for step in range(ROUNDS):
                total, upwind = around(state)
                centre = state[1:-1]
                d, c, l, h = (t[step : t.shape[0] - step, lo:hi] for t in fine_wide)
                state = centre + d * (total - 6.0 * centre) - c * (centre - upwind) - l * centre + h
            states[i] = state

    elements = []
    for i, (lo, hi) in enumerate(bounds):
        total, upwind = around(firsts[i][ROUNDS - 1 : ROUNDS + planes + 1])
        o, s, w = coarse_factors(*(x[:, lo:hi] for x in fine_terms[:3]))
        old = o * starts[i] + s * total + w * upwind
        element = jnp.where(slot > 0, states[i] - old, states[i])
        elements.append(element[:, i * half - lo : (i + 1) * half - lo])
    element = jnp.concatenate(elements, axis=1)

    line = slot * part - halo + lax.broadcasted_iota(jnp.int32, (1, window, 1), 1)
    place = lax.axis_index("space") * planes - deep + lax.broadcasted_iota(jnp.int32, (planes + 2 * deep, 1, 1), 0)
    inside = (line >= 0) & (line < rows) & (place >= 0) & (place < planes * lax.axis_size("space"))
    coarse_terms = coarse_factors(*coarse_wide, inside=inside.astype(jnp.float32))

    blocks = jnp.pad(element, ((0, 0), (halo, halo), (0, 0))).reshape(planes, -1, part, lanes)
    widened = jnp.concatenate([blocks[:, :-1], blocks[:, 1:]], axis=2)
    terms = lax.all_to_all(widened.transpose(1, 0, 2, 3), "tm", 0, 0, tiled=True)

    depth = [SPAN] + [(SPAN - n) % SPAN for n in range(1, slices)]
    before, after = exchanged(
        jnp.concatenate([terms[n, :k] for n, k in enumerate(depth) if k]),
        jnp.concatenate([terms[n, planes - k :] for n, k in enumerate(depth) if k]),
        even,
    )
    offsets = [sum(depth[:n]) for n in range(slices)]

    def term(n):
        k, o = depth[n], offsets[n]
        return jnp.concatenate([before[o : o + k], terms[n], after[o : o + k]]) if k else terms[n]

    state = term(0)
    ends = [terms[0]]
    for n in range(1, slices):
        if n > 1 and n % SPAN == 1:
            low, high = exchanged(state, state, even)
            state = jnp.concatenate([low, state, high])
        k = depth[n]
        trim = deep - k
        o, s, w = (t[trim : t.shape[0] - trim] for t in coarse_terms)
        total, upwind = around(state)
        state = o * state[1:-1] + s * total + w * upwind + term(n)
        ends.append(state[k : k + planes])

    ends = jnp.stack(ends)[:, :, halo : halo + part]
    back = lax.all_to_all(ends, "tm", 0, 0, tiled=True)
    end_state = back.transpose(1, 0, 2, 3).reshape(planes, rows, lanes)
    arrived = lax.ppermute(end_state, "tm", [(i, i + 1) for i in range(slices - 1)])
    following = jnp.where(slot == 0, start, arrived)
    return end_state[None], following[None]


def solution(mesh):
    return jax.shard_map(
        on_device,
        mesh=mesh,
        in_specs=(
            P("tm", "space", None, None),
            P("space", None, None),
            P("space", None, None),
            P("space", None, None),
            P("space", None, None),
        ),
        out_specs=(P("tm", "space", None, None), P("tm", "space", None, None)),
        check_vma=False,
    )
```

```python
import jax
import jax.numpy as jnp
from jax import lax
from jax.sharding import PartitionSpec as P

FINE = 8
SPAN = 4
ROUNDS = 2


def swaps(pairs):
    return [route for a, b in pairs for route in ((a, b), (b, a))]


def beside_pairs():
    return swaps([(i, i + 1) for i in range(0, lax.axis_size("space") - 1, 2)])


def exchanged(low, high, even):
    devices = lax.axis_size("space")
    far = swaps([(i, i + 1) for i in range(1, devices - 1, 2)])
    across = lax.ppermute(jnp.where(even, low, high), "space", far)
    beside = lax.ppermute(jnp.where(even, high, low), "space", beside_pairs())
    return jnp.where(even, across, beside), jnp.where(even, beside, across)


def around(wide):
    padded = jnp.pad(wide, ((0, 0), (1, 1), (1, 1)))
    total = padded[2:, 1:-1, 1:-1] + padded[:-2, 1:-1, 1:-1]
    total = total + padded[1:-1, 2:, 1:-1] + padded[1:-1, :-2, 1:-1]
    total = total + padded[1:-1, 1:-1, 2:] + padded[1:-1, 1:-1, :-2]
    return total, wide[:-2]


def on_device(slice_starts, diffusion, courant, loss, heating):
    start = slice_starts[0]
    planes, rows, lanes = start.shape
    slices = lax.axis_size("tm")
    slot = lax.axis_index("tm")
    even = lax.axis_index("space") % 2 == 0
    part = rows // slices
    halo = slices
    window = part + 2 * halo

    denom = 1.0 + FINE * (6.0 * diffusion + courant + loss)
    own = 1.0 / denom
    side = FINE * diffusion / denom
    west = FINE * courant / denom

    edge = ROUNDS - 1

    def flat(*arrays):
        return jnp.concatenate([a.reshape(-1, lanes) for a in arrays])

    raw = (diffusion, courant, loss, heating)
    before, after = exchanged(flat(*(x[:edge] for x in raw)), flat(*(x[planes - edge :] for x in raw)), even)
    before, after = (x.reshape(4, edge, rows, lanes) for x in (before, after))
    fine_terms = [jnp.concatenate([before[i], raw[i], after[i]]) for i in range(4)]

    state = start
    first = None
    for _ in range(FINE // ROUNDS):
        before, after = exchanged(state[:ROUNDS], state[planes - ROUNDS :], even)
        state = jnp.concatenate([before, state, after])
        if first is None:
            first = state[ROUNDS - 1 : ROUNDS + planes + 1]
        for step in range(ROUNDS):
            total, upwind = around(state)
            centre = state[1:-1]
            trim = step
            d, c, l, h = (t[trim : t.shape[0] - trim] for t in fine_terms)
            state = centre + d * (total - 6.0 * centre) - c * (centre - upwind) - l * centre + h
    total, upwind = around(first)
    coarse_old = own * start + side * total + west * upwind
    element = jnp.where(slot > 0, state - coarse_old, state)

    blocks = jnp.pad(element, ((0, 0), (halo, halo), (0, 0))).reshape(planes, -1, part, lanes)
    widened = jnp.concatenate([blocks[:, :-1], blocks[:, 1:]], axis=2)
    terms = lax.all_to_all(widened.transpose(1, 0, 2, 3), "tm", 0, 0, tiled=True)

    last = slices - 2
    groups = [(g, min(g + SPAN, last)) for g in range(0, last, SPAN)]
    width = {g: end - g + (end == last) for g, end in groups}
    depth = [0] * slices
    for g, end in groups:
        for n in range(g, end + 1):
            depth[n] = width[g] - (n - g)
    deep = SPAN - 1
    inner = [0 if n in width and n else depth[n] for n in range(last + 1)]
    tall = jnp.pad(jnp.stack([own, side, west]), ((0, 0), (0, 0), (halo, halo), (0, 0)))
    factors = lax.dynamic_slice_in_dim(tall, slot * part, window, axis=2)
    before, after = exchanged(
        jnp.concatenate([terms[n, :k] for n, k in enumerate(inner) if k] + [factors[i, :deep] for i in range(3)]),
        jnp.concatenate([terms[n, planes - k :] for n, k in enumerate(inner) if k] + [factors[i, planes - deep :] for i in range(3)]),
        even,
    )
    offsets = [sum(inner[:n]) for n in range(last + 2)]

    def term(n):
        k, o = inner[n], offsets[n]
        return jnp.concatenate([before[o : o + k], terms[n], after[o : o + k]]) if k else terms[n]

    def factor(i):
        o = offsets[last + 1] + i * deep
        return jnp.concatenate([before[o : o + deep], factors[i], after[o : o + deep]])

    coarse_terms = [factor(i) for i in range(3)]
    state = term(0)
    sent = [jnp.zeros((planes + 1, part, lanes), state.dtype)]
    for n in range(last + 1):
        if n:
            k = inner[n]
            trim = deep - k
            o, s, w = (t[trim : t.shape[0] - trim] for t in coarse_terms)
            wide = state[depth[n - 1] - 1 - k : state.shape[0] - (depth[n - 1] - 1 - k)]
            total, upwind = around(wide)
            state = o * wide[1:-1] + s * total + w * upwind + term(n)
            if n in width:
                k = width[n]
                low, high = exchanged(state[:k], state[planes - k :], even)
                state = jnp.concatenate([low, state, high])
        k = depth[n]
        kept = state[:, halo : halo + part]
        sent.append(jnp.concatenate([kept[k : k + planes], jnp.where(even, kept[k - 1 : k], kept[k + planes : k + planes + 1])]))

    back = lax.all_to_all(jnp.stack(sent), "tm", 0, 0, tiled=True)
    arrived = back.transpose(1, 0, 2, 3).reshape(planes + 1, rows, lanes)
    following, across = arrived[:planes], arrived[planes:]
    beside = lax.ppermute(jnp.where(even, following[planes - 1 :], following[:1]), "space", beside_pairs())
    low, high = jnp.where(even, across, beside), jnp.where(even, beside, across)
    total, upwind = around(jnp.concatenate([low, following, high]))
    end_state = jnp.where(slot > 0, own * following + side * total + west * upwind, 0.0) + element
    following = jnp.where(slot == 0, start, following)
    return end_state[None], following[None]


def solution(mesh):
    return jax.shard_map(
        on_device,
        mesh=mesh,
        in_specs=(
            P("tm", "space", None, None),
            P("space", None, None),
            P("space", None, None),
            P("space", None, None),
            P("space", None, None),
        ),
        out_specs=(P("tm", "space", None, None), P("tm", "space", None, None)),
        check_vma=False,
    )
```

```python
import jax
import jax.numpy as jnp
from jax import lax
from jax.sharding import PartitionSpec as P

FINE = 8
SPAN = 4
ROUNDS = 2


def swaps(pairs):
    return [route for a, b in pairs for route in ((a, b), (b, a))]


def beside_pairs():
    return swaps([(i, i + 1) for i in range(0, lax.axis_size("space") - 1, 2)])


def exchanged(low, high, even):
    devices = lax.axis_size("space")
    far = swaps([(i, i + 1) for i in range(1, devices - 1, 2)])
    across = lax.ppermute(jnp.where(even, low, high), "space", far)
    beside = lax.ppermute(jnp.where(even, high, low), "space", beside_pairs())
    return jnp.where(even, across, beside), jnp.where(even, beside, across)


def around(wide):
    padded = jnp.pad(wide, ((0, 0), (1, 1), (1, 1)))
    total = padded[2:, 1:-1, 1:-1] + padded[:-2, 1:-1, 1:-1]
    total = total + padded[1:-1, 2:, 1:-1] + padded[1:-1, :-2, 1:-1]
    total = total + padded[1:-1, 1:-1, 2:] + padded[1:-1, 1:-1, :-2]
    return total, wide[:-2]


def on_device(slice_starts, diffusion, courant, loss, heating):
    start = slice_starts[0]
    planes, rows, lanes = start.shape
    slices = lax.axis_size("tm")
    slot = lax.axis_index("tm")
    even = lax.axis_index("space") % 2 == 0
    part = rows // slices
    halo = slices
    window = part + 2 * halo

    denom = 1.0 + FINE * (6.0 * diffusion + courant + loss)
    own = 1.0 / denom
    side = FINE * diffusion / denom
    west = FINE * courant / denom

    edge = ROUNDS - 1

    def flat(*arrays):
        return jnp.concatenate([a.reshape(-1, lanes) for a in arrays])

    raw = (diffusion, courant, loss, heating)
    before, after = exchanged(flat(*(x[:edge] for x in raw)), flat(*(x[planes - edge :] for x in raw)), even)
    before, after = (x.reshape(4, edge, rows, lanes) for x in (before, after))
    fine_terms = [jnp.concatenate([before[i], raw[i], after[i]]) for i in range(4)]

    state = start
    first = None
    for _ in range(FINE // ROUNDS):
        before, after = exchanged(state[:ROUNDS], state[planes - ROUNDS :], even)
        state = jnp.concatenate([before, state, after])
        if first is None:
            first = state[ROUNDS - 1 : ROUNDS + planes + 1]
        for step in range(ROUNDS):
            total, upwind = around(state)
            centre = state[1:-1]
            trim = step
            d, c, l, h = (t[trim : t.shape[0] - trim] for t in fine_terms)
            state = centre + d * (total - 6.0 * centre) - c * (centre - upwind) - l * centre + h
    total, upwind = around(first)
    coarse_old = own * start + side * total + west * upwind
    element = jnp.where(slot > 0, state - coarse_old, state)

    blocks = jnp.pad(element, ((0, 0), (halo, halo), (0, 0))).reshape(planes, -1, part, lanes)
    widened = jnp.concatenate([blocks[:, :-1], blocks[:, 1:]], axis=2)
    tall = jnp.pad(jnp.stack([own, side, west]), ((0, 0), (0, 0), (halo, halo), (0, 0)))
    factors = lax.dynamic_slice_in_dim(tall, slot * part, window, axis=2)
    widened, element, factors, own, side, west, start = lax.optimization_barrier((widened, element, factors, own, side, west, start))
    terms = lax.all_to_all(widened.transpose(1, 0, 2, 3), "tm", 0, 0, tiled=True)
    terms, element, factors, own, side, west, start = lax.optimization_barrier((terms, element, factors, own, side, west, start))

    last = slices - 2
    groups = [(g, min(g + SPAN, last)) for g in range(0, last, SPAN)]
    width = {g: end - g + (end == last) for g, end in groups}
    depth = [0] * slices
    for g, end in groups:
        for n in range(g, end + 1):
            depth[n] = width[g] - (n - g)
    deep = SPAN - 1
    inner = [0 if n in width and n else depth[n] for n in range(last + 1)]
    before, after = exchanged(
        jnp.concatenate([terms[n, :k] for n, k in enumerate(inner) if k] + [factors[i, :deep] for i in range(3)]),
        jnp.concatenate([terms[n, planes - k :] for n, k in enumerate(inner) if k] + [factors[i, planes - deep :] for i in range(3)]),
        even,
    )
    offsets = [sum(inner[:n]) for n in range(last + 2)]

    def term(n):
        k, o = inner[n], offsets[n]
        return jnp.concatenate([before[o : o + k], terms[n], after[o : o + k]]) if k else terms[n]

    def factor(i):
        o = offsets[last + 1] + i * deep
        return jnp.concatenate([before[o : o + deep], factors[i], after[o : o + deep]])

    coarse_terms = [factor(i) for i in range(3)]
    state = term(0)
    sent = [jnp.zeros((planes + 1, part, lanes), state.dtype)]
    for n in range(last + 1):
        if n:
            k = inner[n]
            trim = deep - k
            o, s, w = (t[trim : t.shape[0] - trim] for t in coarse_terms)
            wide = state[depth[n - 1] - 1 - k : state.shape[0] - (depth[n - 1] - 1 - k)]
            total, upwind = around(wide)
            state = o * wide[1:-1] + s * total + w * upwind + term(n)
            if n in width:
                k = width[n]
                low, high = exchanged(state[:k], state[planes - k :], even)
                state = jnp.concatenate([low, state, high])
        k = depth[n]
        kept = state[:, halo : halo + part]
        sent.append(jnp.concatenate([kept[k : k + planes], jnp.where(even, kept[k - 1 : k], kept[k + planes : k + planes + 1])]))

    sent, element, own, side, west, start, slot, even = lax.optimization_barrier(
        (jnp.stack(sent), element, own, side, west, start, slot, even)
    )
    back = lax.all_to_all(sent, "tm", 0, 0, tiled=True)
    back, element, own, side, west, start, slot, even = lax.optimization_barrier((back, element, own, side, west, start, slot, even))
    arrived = back.transpose(1, 0, 2, 3).reshape(planes + 1, rows, lanes)
    following, across = arrived[:planes], arrived[planes:]
    beside = lax.ppermute(jnp.where(even, following[planes - 1 :], following[:1]), "space", beside_pairs())
    low, high = jnp.where(even, across, beside), jnp.where(even, beside, across)
    total, upwind = around(jnp.concatenate([low, following, high]))
    end_state = jnp.where(slot > 0, own * following + side * total + west * upwind, 0.0) + element
    following = jnp.where(slot == 0, start, following)
    return end_state[None], following[None]


def solution(mesh):
    return jax.shard_map(
        on_device,
        mesh=mesh,
        in_specs=(
            P("tm", "space", None, None),
            P("space", None, None),
            P("space", None, None),
            P("space", None, None),
            P("space", None, None),
        ),
        out_specs=(P("tm", "space", None, None), P("tm", "space", None, None)),
        check_vma=False,
    )
```

```python
import jax
import jax.numpy as jnp
from jax import lax
from jax.sharding import PartitionSpec as P

FINE = 8
SPAN = 4
ROUNDS = 2
HALO = 8
OLD_TURN = 1


def swaps(pairs):
    return [route for a, b in pairs for route in ((a, b), (b, a))]


def beside_pairs():
    return swaps([(i, i + 1) for i in range(0, lax.axis_size("space") - 1, 2)])


def across_pairs():
    return swaps([(i, i + 1) for i in range(1, lax.axis_size("space") - 1, 2)])


def exchanged(low, high, even):
    across = lax.ppermute(jnp.where(even, low, high), "space", across_pairs())
    beside = lax.ppermute(jnp.where(even, high, low), "space", beside_pairs())
    return jnp.where(even, across, beside), jnp.where(even, beside, across)


def around(wide):
    padded = jnp.pad(wide, ((0, 0), (1, 1), (1, 1)))
    total = padded[2:, 1:-1, 1:-1] + padded[:-2, 1:-1, 1:-1]
    total = total + padded[1:-1, 2:, 1:-1] + padded[1:-1, :-2, 1:-1]
    total = total + padded[1:-1, 1:-1, 2:] + padded[1:-1, 1:-1, :-2]
    return total, wide[:-2]


def fine_step(wide, terms):
    d, c, l, h = terms
    total, upwind = around(wide)
    centre = wide[1:-1]
    return centre + d * (total - 6.0 * centre) - c * (centre - upwind) - l * centre + h


def coarse_linear(wide, terms):
    d, c, l = terms
    total, upwind = around(wide)
    return (wide[1:-1] + FINE * (d * total + c * upwind)) / (1.0 + FINE * (6.0 * d + c + l))


def snake(index):
    turned = (index // 2) % 2
    return index + turned * (1 - 2 * (index % 2))


def on_device(slice_starts, diffusion, courant, loss, heating):
    start = slice_starts[0]
    planes, rows, lanes = start.shape
    slices = lax.axis_size("tm")
    slot = lax.axis_index("tm")
    even = lax.axis_index("space") % 2 == 0
    part = rows // slices
    window = part + 2 * HALO
    order = [snake(i) for i in range(slices)]
    raw = (diffusion, courant, loss, heating)

    def flat(*arrays):
        return jnp.concatenate([a.reshape(-1, lanes) for a in arrays])

    edge = ROUNDS - 1
    before, after = exchanged(flat(*(x[:edge] for x in raw)), flat(*(x[planes - edge :] for x in raw)), even)
    before, after = before.reshape(4, edge, rows, lanes), after.reshape(4, edge, rows, lanes)
    fine_terms = [jnp.concatenate([before[i], raw[i], after[i]]) for i in range(4)]

    state = start
    for turn in range(FINE // ROUNDS):
        low, high = state[:ROUNDS], state[planes - ROUNDS :]
        if turn == OLD_TURN:
            low, high, first = lax.optimization_barrier((low, high, first))
        low, high = exchanged(low, high, even)
        if turn == OLD_TURN:
            old = coarse_linear(first, raw[:3])
        state = jnp.concatenate([low, state, high])
        if turn == 0:
            first = state[ROUNDS - 1 : ROUNDS + planes + 1]
        for step in range(ROUNDS):
            state = fine_step(state, [t[step : t.shape[0] - step] for t in fine_terms])
    element = jnp.where(slot > 0, state - old, state)

    place = snake(slot)
    line = place * part - HALO + lax.broadcasted_iota(jnp.int32, (1, window, 1), 1)
    inside = ((line >= 0) & (line < rows)).astype(jnp.float32)
    d, c, l = (
        lax.dynamic_slice_in_dim(jnp.pad(x, ((0, 0), (HALO, HALO), (0, 0))), place * part, window, axis=1) for x in raw[:3]
    )
    scale = inside / (1.0 + FINE * (6.0 * d + c + l))
    factors = jnp.stack([scale, FINE * d * scale, FINE * c * scale])

    tall = jnp.pad(element, ((0, 0), (HALO, HALO), (0, 0)))
    widened = jnp.stack([tall[:, p * part : p * part + window] for p in order])
    widened, element, factors, slot, even, place = lax.optimization_barrier((widened, element, factors, slot, even, place))
    terms = lax.all_to_all(widened, "tm", 0, 0, tiled=True)
    terms, element, factors, slot, even, place = lax.optimization_barrier((terms, element, factors, slot, even, place))

    last = slices - 2
    groups = [(g, min(g + SPAN, last)) for g in range(0, last, SPAN)]
    width = {g: end - g + (end == last) for g, end in groups}
    depth = [0] * slices
    for g, end in groups:
        for n in range(g, end + 1):
            depth[n] = width[g] - (n - g)
    deep = SPAN - 1
    inner = [0 if n in width and n else depth[n] for n in range(last + 1)]
    before, after = exchanged(
        jnp.concatenate([terms[n, :k] for n, k in enumerate(inner) if k] + [factors[i, :deep] for i in range(3)]),
        jnp.concatenate([terms[n, planes - k :] for n, k in enumerate(inner) if k] + [factors[i, planes - deep :] for i in range(3)]),
        even,
    )
    offsets = [sum(inner[:n]) for n in range(last + 2)]

    def term(n):
        k, o = inner[n], offsets[n]
        return jnp.concatenate([before[o : o + k], terms[n], after[o : o + k]]) if k else terms[n]

    def factor(i):
        o = offsets[last + 1] + i * deep
        return jnp.concatenate([before[o : o + deep], factors[i], after[o : o + deep]])

    def rows_exchanged(state):
        first_of_pair = place % 2 == 0
        top, bottom = state[:, HALO : 2 * HALO], state[:, part : part + HALO]
        within = swaps([(order[i], order[i + 1]) for i in range(0, slices - 1, 2)])
        between = swaps([(order[i], order[i + 1]) for i in range(1, slices - 1, 2)])
        inner_rows = lax.ppermute(jnp.where(first_of_pair, bottom, top), "tm", within)
        outer_rows = lax.ppermute(jnp.where(first_of_pair, top, bottom), "tm", between)
        above = jnp.where(first_of_pair, outer_rows, inner_rows)
        below = jnp.where(first_of_pair, inner_rows, outer_rows)
        return jnp.concatenate([above, state[:, HALO : HALO + part], below], axis=1)

    coarse_terms = [factor(i) for i in range(3)]
    state = term(0)
    sent = [jnp.zeros((planes + 1, part, lanes), state.dtype)]
    for n in range(last + 1):
        if n:
            k = inner[n]
            trim = deep - k
            o, s, w = (t[trim : t.shape[0] - trim] for t in coarse_terms)
            wide = state[depth[n - 1] - 1 - k : state.shape[0] - (depth[n - 1] - 1 - k)]
            total, upwind = around(wide)
            state = o * wide[1:-1] + s * total + w * upwind + term(n)
            if n in width:
                if n % HALO == 0:
                    state = rows_exchanged(state)
                k = width[n]
                low, high = exchanged(state[:k], state[planes - k :], even)
                state = jnp.concatenate([low, state, high])
        k = depth[n]
        kept = state[:, HALO : HALO + part]
        sent.append(jnp.concatenate([kept[k : k + planes], jnp.where(even, kept[k - 1 : k], kept[k + planes : k + planes + 1])]))

    sent, element, slot, even = lax.optimization_barrier((jnp.stack(sent), element, slot, even))
    back = lax.all_to_all(sent, "tm", 0, 0, tiled=True)
    back, element, slot, even = lax.optimization_barrier((back, element, slot, even))
    arrived = jnp.concatenate([back[i] for i in order], axis=1)
    following, across = arrived[:planes], arrived[planes:]
    beside = lax.ppermute(jnp.where(even, following[planes - 1 :], following[:1]), "space", beside_pairs())
    low, high = jnp.where(even, across, beside), jnp.where(even, beside, across)
    coarse = coarse_linear(jnp.concatenate([low, following, high]), raw[:3])
    end_state = jnp.where(slot > 0, coarse, 0.0) + element
    following = jnp.where(slot == 0, start, following)
    return end_state[None], following[None]


def solution(mesh):
    return jax.shard_map(
        on_device,
        mesh=mesh,
        in_specs=(
            P("tm", "space", None, None),
            P("space", None, None),
            P("space", None, None),
            P("space", None, None),
            P("space", None, None),
        ),
        out_specs=(P("tm", "space", None, None), P("tm", "space", None, None)),
        check_vma=False,
    )
```

```python
import jax
import jax.numpy as jnp
from jax import lax
from jax.sharding import PartitionSpec as P

FINE = 8
SPAN = 4
ROUNDS = 2
HALO = 8
OLD_TURN = 1


def swaps(pairs):
    return [route for a, b in pairs for route in ((a, b), (b, a))]


def beside_pairs():
    return swaps([(i, i + 1) for i in range(0, lax.axis_size("space") - 1, 2)])


def across_pairs():
    return swaps([(i, i + 1) for i in range(1, lax.axis_size("space") - 1, 2)])


def exchanged(low, high, even):
    across = lax.ppermute(jnp.where(even, low, high), "space", across_pairs())
    beside = lax.ppermute(jnp.where(even, high, low), "space", beside_pairs())
    return jnp.where(even, across, beside), jnp.where(even, beside, across)


def around(wide):
    padded = jnp.pad(wide, ((0, 0), (1, 1), (1, 1)))
    total = padded[2:, 1:-1, 1:-1] + padded[:-2, 1:-1, 1:-1]
    total = total + padded[1:-1, 2:, 1:-1] + padded[1:-1, :-2, 1:-1]
    total = total + padded[1:-1, 1:-1, 2:] + padded[1:-1, 1:-1, :-2]
    return total, wide[:-2]


def fine_step(wide, terms):
    d, c, l, h = terms
    total, upwind = around(wide)
    centre = wide[1:-1]
    return centre + d * (total - 6.0 * centre) - c * (centre - upwind) - l * centre + h


def coarse_linear(wide, terms):
    d, c, l = terms
    total, upwind = around(wide)
    return (wide[1:-1] + FINE * (d * total + c * upwind)) / (1.0 + FINE * (6.0 * d + c + l))


def snake(index):
    turned = (index // 2) % 2
    return index + turned * (1 - 2 * (index % 2))


def on_device(slice_starts, diffusion, courant, loss, heating):
    start = slice_starts[0]
    planes, rows, lanes = start.shape
    slices = lax.axis_size("tm")
    slot = lax.axis_index("tm")
    even = lax.axis_index("space") % 2 == 0
    part = rows // slices
    window = part + 2 * HALO
    order = [snake(i) for i in range(slices)]
    raw = (diffusion, courant, loss, heating)

    def flat(*arrays):
        return jnp.concatenate([a.reshape(-1, lanes) for a in arrays])

    edge = ROUNDS - 1
    before, after = exchanged(flat(*(x[:edge] for x in raw)), flat(*(x[planes - edge :] for x in raw)), even)
    before, after = before.reshape(4, edge, rows, lanes), after.reshape(4, edge, rows, lanes)
    fine_terms = [jnp.concatenate([before[i], raw[i], after[i]]) for i in range(4)]

    state = start
    for turn in range(FINE // ROUNDS):
        low, high = state[:ROUNDS], state[planes - ROUNDS :]
        if turn == OLD_TURN:
            low, high, first = lax.optimization_barrier((low, high, first))
        low, high = exchanged(low, high, even)
        if turn == OLD_TURN:
            old = coarse_linear(first, raw[:3])
            low, high, old = lax.optimization_barrier((low, high, old))
        state = jnp.concatenate([low, state, high])
        if turn == 0:
            first = state[ROUNDS - 1 : ROUNDS + planes + 1]
        for step in range(ROUNDS):
            state = fine_step(state, [t[step : t.shape[0] - step] for t in fine_terms])
    element = jnp.where(slot > 0, state - old, state)

    place = snake(slot)
    line = place * part - HALO + lax.broadcasted_iota(jnp.int32, (1, window, 1), 1)
    inside = ((line >= 0) & (line < rows)).astype(jnp.float32)
    d, c, l = (
        lax.dynamic_slice_in_dim(jnp.pad(x, ((0, 0), (HALO, HALO), (0, 0))), place * part, window, axis=1) for x in raw[:3]
    )
    scale = inside / (1.0 + FINE * (6.0 * d + c + l))
    factors = jnp.stack([scale, FINE * d * scale, FINE * c * scale])

    tall = jnp.pad(element, ((0, 0), (HALO, HALO), (0, 0)))
    widened = jnp.stack([tall[:, p * part : p * part + window] for p in order])
    widened, element, factors, slot, even, place = lax.optimization_barrier((widened, element, factors, slot, even, place))
    terms = lax.all_to_all(widened, "tm", 0, 0, tiled=True)
    terms, element, factors, slot, even, place = lax.optimization_barrier((terms, element, factors, slot, even, place))

    last = slices - 2
    groups = [(g, min(g + SPAN, last)) for g in range(0, last, SPAN)]
    width = {g: end - g + (end == last) for g, end in groups}
    depth = [0] * slices
    for g, end in groups:
        for n in range(g, end + 1):
            depth[n] = width[g] - (n - g)
    deep = SPAN - 1
    inner = [0 if n in width and n else depth[n] for n in range(last + 1)]
    before, after = exchanged(
        jnp.concatenate([terms[n, :k] for n, k in enumerate(inner) if k] + [factors[i, :deep] for i in range(3)]),
        jnp.concatenate([terms[n, planes - k :] for n, k in enumerate(inner) if k] + [factors[i, planes - deep :] for i in range(3)]),
        even,
    )
    offsets = [sum(inner[:n]) for n in range(last + 2)]

    def term(n):
        k, o = inner[n], offsets[n]
        return jnp.concatenate([before[o : o + k], terms[n], after[o : o + k]]) if k else terms[n]

    def factor(i):
        o = offsets[last + 1] + i * deep
        return jnp.concatenate([before[o : o + deep], factors[i], after[o : o + deep]])

    def rows_exchanged(state):
        first_of_pair = place % 2 == 0
        top, bottom = state[:, HALO : 2 * HALO], state[:, part : part + HALO]
        within = swaps([(order[i], order[i + 1]) for i in range(0, slices - 1, 2)])
        between = swaps([(order[i], order[i + 1]) for i in range(1, slices - 1, 2)])
        inner_rows = lax.ppermute(jnp.where(first_of_pair, bottom, top), "tm", within)
        outer_rows = lax.ppermute(jnp.where(first_of_pair, top, bottom), "tm", between)
        above = jnp.where(first_of_pair, outer_rows, inner_rows)
        below = jnp.where(first_of_pair, inner_rows, outer_rows)
        return jnp.concatenate([above, state[:, HALO : HALO + part], below], axis=1)

    coarse_terms = [factor(i) for i in range(3)]
    state = term(0)
    sent = [jnp.zeros((planes + 1, part, lanes), state.dtype)]
    for n in range(last + 1):
        if n:
            k = inner[n]
            trim = deep - k
            o, s, w = (t[trim : t.shape[0] - trim] for t in coarse_terms)
            wide = state[depth[n - 1] - 1 - k : state.shape[0] - (depth[n - 1] - 1 - k)]
            total, upwind = around(wide)
            state = o * wide[1:-1] + s * total + w * upwind + term(n)
            if n in width:
                if n % HALO == 0:
                    state = rows_exchanged(state)
                k = width[n]
                low, high = exchanged(state[:k], state[planes - k :], even)
                state = jnp.concatenate([low, state, high])
        k = depth[n]
        kept = state[:, HALO : HALO + part]
        sent.append(jnp.concatenate([kept[k : k + planes], jnp.where(even, kept[k - 1 : k], kept[k + planes : k + planes + 1])]))

    turned = lax.broadcasted_iota(jnp.int32, (slices // 2, 1, 1, 1, 1), 0) % 2
    sent, element, slot, even, turned = lax.optimization_barrier((jnp.stack(sent), element, slot, even, turned))
    back = lax.all_to_all(sent, "tm", 0, 0, tiled=True)
    back, element, slot, even, turned = lax.optimization_barrier((back, element, slot, even, turned))
    pairs = back.reshape((slices // 2, 2) + back.shape[1:])
    back = jnp.where(turned == 1, pairs[:, ::-1], pairs).reshape(back.shape)
    arrived = back.transpose(1, 0, 2, 3).reshape(planes + 1, rows, lanes)
    following, across = arrived[:planes], arrived[planes:]
    beside = lax.ppermute(jnp.where(even, following[planes - 1 :], following[:1]), "space", beside_pairs())
    low, high = jnp.where(even, across, beside), jnp.where(even, beside, across)
    coarse = coarse_linear(jnp.concatenate([low, following, high]), raw[:3])
    end_state = jnp.where(slot > 0, coarse, 0.0) + element
    following = jnp.where(slot == 0, start, following)
    return end_state[None], following[None]


def solution(mesh):
    return jax.shard_map(
        on_device,
        mesh=mesh,
        in_specs=(
            P("tm", "space", None, None),
            P("space", None, None),
            P("space", None, None),
            P("space", None, None),
            P("space", None, None),
        ),
        out_specs=(P("tm", "space", None, None), P("tm", "space", None, None)),
        check_vma=False,
    )
```

```python
import jax
import jax.numpy as jnp
from jax import lax
from jax.experimental import pallas as pl
from jax.experimental.pallas import tpu as pltpu
from jax.sharding import PartitionSpec as P

FINE = 8
SPAN = 4
ROUNDS = 2
HALO = 8
OLD_TURN = 1


def swaps(pairs):
    return [route for a, b in pairs for route in ((a, b), (b, a))]


def beside_pairs():
    return swaps([(i, i + 1) for i in range(0, lax.axis_size("space") - 1, 2)])


def across_pairs():
    return swaps([(i, i + 1) for i in range(1, lax.axis_size("space") - 1, 2)])


def exchanged(low, high, even):
    across = lax.ppermute(jnp.where(even, low, high), "space", across_pairs())
    beside = lax.ppermute(jnp.where(even, high, low), "space", beside_pairs())
    return jnp.where(even, across, beside), jnp.where(even, beside, across)


def around(wide):
    padded = jnp.pad(wide, ((0, 0), (1, 1), (1, 1)))
    total = padded[2:, 1:-1, 1:-1] + padded[:-2, 1:-1, 1:-1]
    total = total + padded[1:-1, 2:, 1:-1] + padded[1:-1, :-2, 1:-1]
    total = total + padded[1:-1, 1:-1, 2:] + padded[1:-1, 1:-1, :-2]
    return total, wide[:-2]


def fine_step(wide, terms):
    d, c, l, h = terms
    total, upwind = around(wide)
    centre = wide[1:-1]
    return centre + d * (total - 6.0 * centre) - c * (centre - upwind) - l * centre + h


def coarse_linear(wide, terms):
    d, c, l = terms
    total, upwind = around(wide)
    return (wide[1:-1] + FINE * (d * total + c * upwind)) / (1.0 + FINE * (6.0 * d + c + l))


def edges_packed(terms, factors, plan):
    planes, rows, lanes = terms.shape[1:]
    pieces = [(g, o, k, f, i) for g, group in enumerate(plan) for o, (f, i, k) in zip(offsets_of(group), group)]

    def kernel(terms_ref, factors_ref, *refs):
        outs, sems = refs[:-1], refs[-1]
        odd = lax.axis_index("space") % 2
        copies = []
        for j, (g, o, k, f, i) in enumerate(pieces):
            source = (factors_ref if f else terms_ref).at[i]
            for side in range(2):
                at = (odd if side == 0 else 1 - odd) * (planes - k)
                copies.append(
                    pltpu.make_async_copy(source.at[pl.ds(at, k)], outs[2 * g + side].at[pl.ds(o, k)], sems.at[2 * j + side])
                )
        for copy in copies:
            copy.start()
        for copy in copies:
            copy.wait()

    sizes = [sum(k for _, _, k in group) for group in plan]
    shapes = [jax.ShapeDtypeStruct((n, rows, lanes), terms.dtype) for n in sizes for _ in range(2)]
    anywhere = pl.BlockSpec(memory_space=pl.ANY)
    outs = pl.pallas_call(
        kernel,
        name="edges_packed",
        out_shape=shapes,
        in_specs=[anywhere, anywhere],
        out_specs=[anywhere] * len(shapes),
        scratch_shapes=[pltpu.SemaphoreType.DMA((2 * len(pieces),))],
        compiler_params=pltpu.CompilerParams(vmem_limit_bytes=1 << 20),
    )(terms, factors)
    return [(outs[2 * g], outs[2 * g + 1]) for g in range(len(plan))]


def offsets_of(group):
    out = [0]
    for _, _, k in group:
        out.append(out[-1] + k)
    return out


def snake(index):
    turned = (index // 2) % 2
    return index + turned * (1 - 2 * (index % 2))


def on_device(slice_starts, diffusion, courant, loss, heating):
    start = slice_starts[0]
    planes, rows, lanes = start.shape
    slices = lax.axis_size("tm")
    slot = lax.axis_index("tm")
    even = lax.axis_index("space") % 2 == 0
    part = rows // slices
    window = part + 2 * HALO
    order = [snake(i) for i in range(slices)]
    raw = (diffusion, courant, loss, heating)

    def flat(*arrays):
        return jnp.concatenate([a.reshape(-1, lanes) for a in arrays])

    edge = ROUNDS - 1
    before, after = exchanged(flat(*(x[:edge] for x in raw)), flat(*(x[planes - edge :] for x in raw)), even)
    before, after = before.reshape(4, edge, rows, lanes), after.reshape(4, edge, rows, lanes)
    fine_terms = [jnp.concatenate([before[i], raw[i], after[i]]) for i in range(4)]

    state = start
    for turn in range(FINE // ROUNDS):
        low, high = state[:ROUNDS], state[planes - ROUNDS :]
        if turn == OLD_TURN:
            low, high, first = lax.optimization_barrier((low, high, first))
        low, high = exchanged(low, high, even)
        if turn == OLD_TURN:
            old = coarse_linear(first, raw[:3])
            low, high, old = lax.optimization_barrier((low, high, old))
        state = jnp.concatenate([low, state, high])
        if turn == 0:
            first = state[ROUNDS - 1 : ROUNDS + planes + 1]
        for step in range(ROUNDS):
            state = fine_step(state, [t[step : t.shape[0] - step] for t in fine_terms])
    element = jnp.where(slot > 0, state - old, state)

    place = snake(slot)
    line = place * part - HALO + lax.broadcasted_iota(jnp.int32, (1, window, 1), 1)
    inside = ((line >= 0) & (line < rows)).astype(jnp.float32)
    d, c, l = (
        lax.dynamic_slice_in_dim(jnp.pad(x, ((0, 0), (HALO, HALO), (0, 0))), place * part, window, axis=1) for x in raw[:3]
    )
    scale = inside / (1.0 + FINE * (6.0 * d + c + l))
    factors = jnp.stack([scale, FINE * d * scale, FINE * c * scale])

    tall = jnp.pad(element, ((0, 0), (HALO, HALO), (0, 0)))
    widened = jnp.stack([tall[:, p * part : p * part + window] for p in order])
    turned = lax.broadcasted_iota(jnp.int32, (slices // 2, 1, 1, 1, 1), 0) % 2
    kept = (element, factors, slot, even, place, turned)
    widened, *kept = lax.optimization_barrier((widened, *kept))
    terms = lax.all_to_all(widened, "tm", 0, 0, tiled=True)
    terms, element, factors, slot, even, place, turned = lax.optimization_barrier((terms, *kept))

    last = slices - 2
    groups = [(g, min(g + SPAN, last)) for g in range(0, last, SPAN)]
    width = {g: end - g + (end == last) for g, end in groups}
    depth = [0] * slices
    for g, end in groups:
        for n in range(g, end + 1):
            depth[n] = width[g] - (n - g)
    deep = SPAN - 1
    inner = [0 if n in width and n else depth[n] for n in range(last + 1)]
    plan = []
    for g, end in groups:
        plan.append([(False, n, inner[n]) for n in range(g if g == 0 else g + 1, min(g + SPAN, last) + 1) if inner[n]])
    plan[0] += [(True, i, deep) for i in range(3)]
    packed = edges_packed(terms, factors, plan)

    def group_exchanged(g, state):
        group = plan[g // SPAN]
        far, near = packed[g // SPAN]
        pieces = [(factors if f else terms)[i] for f, i, _ in group]
        starts_at = offsets_of(group)
        if g:
            k = width[g]
            far = jnp.concatenate([jnp.where(even, state[:k], state[planes - k :]), far])
            near = jnp.concatenate([jnp.where(even, state[planes - k :], state[:k]), near])
            pieces, starts_at = [state] + pieces, [0] + [o + k for o in starts_at]
        far = lax.ppermute(far, "space", across_pairs())
        near = lax.ppermute(near, "space", beside_pairs())
        low, high = jnp.where(even, far, near), jnp.where(even, near, far)
        return [jnp.concatenate([low[o:e], x, high[o:e]]) for x, o, e in zip(pieces, starts_at, starts_at[1:])]

    def rows_exchanged(state):
        first_of_pair = place % 2 == 0
        top, bottom = state[:, HALO : 2 * HALO], state[:, part : part + HALO]
        within = swaps([(order[i], order[i + 1]) for i in range(0, slices - 1, 2)])
        between = swaps([(order[i], order[i + 1]) for i in range(1, slices - 1, 2)])
        inner_rows = lax.ppermute(jnp.where(first_of_pair, bottom, top), "tm", within)
        outer_rows = lax.ppermute(jnp.where(first_of_pair, top, bottom), "tm", between)
        above = jnp.where(first_of_pair, outer_rows, inner_rows)
        below = jnp.where(first_of_pair, inner_rows, outer_rows)
        return jnp.concatenate([above, state[:, HALO : HALO + part], below], axis=1)

    wide_terms = {n: terms[n] for n in range(slices)}
    sent = []
    state = terms[0]
    for n in range(last + 1):
        if n:
            k = inner[n]
            trim = deep - k
            o, s, w = (t[trim : t.shape[0] - trim] for t in coarse_terms)
            wide = state[depth[n - 1] - 1 - k : state.shape[0] - (depth[n - 1] - 1 - k)]
            total, upwind = around(wide)
            state = o * wide[1:-1] + s * total + w * upwind + wide_terms[n]
        if n in width:
            if n and n % HALO == 0:
                state = rows_exchanged(state)
            state, *more = group_exchanged(n, state)
            if n == 0:
                coarse_terms, more = more[-3:], more[:-3]
            for m, x in zip(range(n + 1, last + 1), more):
                wide_terms[m] = x
        k = depth[n]
        kept = state[:, HALO : HALO + part]
        sent.append(jnp.concatenate([kept[k : k + planes], jnp.where(even, kept[k - 1 : k], kept[k + planes : k + planes + 1])]))

    sent, element, slot, even, turned = lax.optimization_barrier((jnp.stack(sent[:1] + sent), element, slot, even, turned))
    back = lax.all_to_all(sent, "tm", 0, 0, tiled=True)
    back, element, slot, even, turned = lax.optimization_barrier((back, element, slot, even, turned))
    pairs = back.reshape((slices // 2, 2) + back.shape[1:])
    back = jnp.where(turned == 1, pairs[:, ::-1], pairs).reshape(back.shape)
    arrived = back.transpose(1, 0, 2, 3).reshape(planes + 1, rows, lanes)
    following, across = arrived[:planes], arrived[planes:]
    beside = lax.ppermute(jnp.where(even, following[planes - 1 :], following[:1]), "space", beside_pairs())
    low, high = jnp.where(even, across, beside), jnp.where(even, beside, across)
    coarse = coarse_linear(jnp.concatenate([low, following, high]), raw[:3])
    end_state = jnp.where(slot > 0, coarse, 0.0) + element
    following = jnp.where(slot == 0, start, following)
    return end_state[None], following[None]


def solution(mesh):
    return jax.shard_map(
        on_device,
        mesh=mesh,
        in_specs=(
            P("tm", "space", None, None),
            P("space", None, None),
            P("space", None, None),
            P("space", None, None),
            P("space", None, None),
        ),
        out_specs=(P("tm", "space", None, None), P("tm", "space", None, None)),
        check_vma=False,
    )
```

```python
import jax
import jax.numpy as jnp
from jax import lax
from jax.experimental import pallas as pl
from jax.experimental.pallas import tpu as pltpu
from jax.sharding import PartitionSpec as P

FINE = 8
SPAN = 4
ROUNDS = 2
HALO = 8
OLD_TURN = 1


def swaps(pairs):
    return [route for a, b in pairs for route in ((a, b), (b, a))]


def beside_pairs():
    return swaps([(i, i + 1) for i in range(0, lax.axis_size("space") - 1, 2)])


def across_pairs():
    return swaps([(i, i + 1) for i in range(1, lax.axis_size("space") - 1, 2)])


def exchanged(low, high, even):
    across = lax.ppermute(jnp.where(even, low, high), "space", across_pairs())
    beside = lax.ppermute(jnp.where(even, high, low), "space", beside_pairs())
    return jnp.where(even, across, beside), jnp.where(even, beside, across)


def around(wide):
    padded = jnp.pad(wide, ((0, 0), (1, 1), (1, 1)))
    total = padded[2:, 1:-1, 1:-1] + padded[:-2, 1:-1, 1:-1]
    total = total + padded[1:-1, 2:, 1:-1] + padded[1:-1, :-2, 1:-1]
    total = total + padded[1:-1, 1:-1, 2:] + padded[1:-1, 1:-1, :-2]
    return total, wide[:-2]


def fine_step(wide, terms):
    d, c, l, h = terms
    total, upwind = around(wide)
    centre = wide[1:-1]
    return centre + d * (total - 6.0 * centre) - c * (centre - upwind) - l * centre + h


def coarse_linear(wide, terms):
    d, c, l = terms
    total, upwind = around(wide)
    return (wide[1:-1] + FINE * (d * total + c * upwind)) / (1.0 + FINE * (6.0 * d + c + l))


def edges_packed(terms, factors, plan):
    planes, rows, lanes = terms.shape[1:]
    pieces = [(g, o, k, f, i) for g, group in enumerate(plan) for o, (f, i, k) in zip(offsets_of(group), group)]

    def kernel(terms_ref, factors_ref, *refs):
        outs, sems = refs[:-1], refs[-1]
        odd = lax.axis_index("space") % 2
        copies = []
        for j, (g, o, k, f, i) in enumerate(pieces):
            source = (factors_ref if f else terms_ref).at[i]
            for side in range(2):
                at = (odd if side == 0 else 1 - odd) * (planes - k)
                copies.append(
                    pltpu.make_async_copy(source.at[pl.ds(at, k)], outs[2 * g + side].at[pl.ds(o, k)], sems.at[2 * j + side])
                )
        for copy in copies:
            copy.start()
        for copy in copies:
            copy.wait()

    sizes = [sum(k for _, _, k in group) for group in plan]
    shapes = [jax.ShapeDtypeStruct((n, rows, lanes), terms.dtype) for n in sizes for _ in range(2)]
    anywhere = pl.BlockSpec(memory_space=pl.ANY)
    outs = pl.pallas_call(
        kernel,
        name="edges_packed",
        out_shape=shapes,
        in_specs=[anywhere, anywhere],
        out_specs=[anywhere] * len(shapes),
        scratch_shapes=[pltpu.SemaphoreType.DMA((2 * len(pieces),))],
        compiler_params=pltpu.CompilerParams(vmem_limit_bytes=1 << 20),
    )(terms, factors)
    return [(outs[2 * g], outs[2 * g + 1]) for g in range(len(plan))]


def offsets_of(group):
    out = [0]
    for _, _, k in group:
        out.append(out[-1] + k)
    return out


def snake(index):
    turned = (index // 2) % 2
    return index + turned * (1 - 2 * (index % 2))


def on_device(slice_starts, diffusion, courant, loss, heating):
    start = slice_starts[0]
    planes, rows, lanes = start.shape
    slices = lax.axis_size("tm")
    slot = lax.axis_index("tm")
    even = lax.axis_index("space") % 2 == 0
    part = rows // slices
    window = part + 2 * HALO
    order = [snake(i) for i in range(slices)]
    raw = (diffusion, courant, loss, heating)

    def flat(*arrays):
        return jnp.concatenate([a.reshape(-1, lanes) for a in arrays])

    edge = ROUNDS - 1
    before, after = exchanged(flat(*(x[:edge] for x in raw)), flat(*(x[planes - edge :] for x in raw)), even)
    before, after = before.reshape(4, edge, rows, lanes), after.reshape(4, edge, rows, lanes)
    fine_terms = lax.optimization_barrier(jnp.concatenate([before, jnp.stack(raw), after], axis=1))
    raw = [x[edge : edge + planes] for x in fine_terms]

    state = start
    for turn in range(FINE // ROUNDS):
        low, high = state[:ROUNDS], state[planes - ROUNDS :]
        if turn == OLD_TURN:
            low, high, first = lax.optimization_barrier((low, high, first))
        low, high = exchanged(low, high, even)
        if turn == OLD_TURN:
            old = coarse_linear(first, raw[:3])
            low, high, old = lax.optimization_barrier((low, high, old))
        state = jnp.concatenate([low, state, high])
        if turn == 0:
            first = state[ROUNDS - 1 : ROUNDS + planes + 1]
        for step in range(ROUNDS):
            state = fine_step(state, [t[step : t.shape[0] - step] for t in fine_terms])
    element = jnp.where(slot > 0, state - old, state)

    place = snake(slot)
    line = place * part - HALO + lax.broadcasted_iota(jnp.int32, (1, window, 1), 1)
    inside = ((line >= 0) & (line < rows)).astype(jnp.float32)
    d, c, l = (
        lax.dynamic_slice_in_dim(jnp.pad(x, ((0, 0), (HALO, HALO), (0, 0))), place * part, window, axis=1) for x in raw[:3]
    )
    scale = inside / (1.0 + FINE * (6.0 * d + c + l))
    factors = jnp.stack([scale, FINE * d * scale, FINE * c * scale])

    tall = jnp.pad(element, ((0, 0), (HALO, HALO), (0, 0)))
    widened = jnp.stack([tall[:, p * part : p * part + window] for p in order])
    turned = lax.broadcasted_iota(jnp.int32, (slices // 2, 1, 1, 1, 1), 0) % 2
    kept = (element, factors, slot, even, place, turned)
    widened, *kept = lax.optimization_barrier((widened, *kept))
    terms = lax.all_to_all(widened, "tm", 0, 0, tiled=True)
    terms, element, factors, slot, even, place, turned = lax.optimization_barrier((terms, *kept))

    last = slices - 2
    groups = [(g, min(g + SPAN, last)) for g in range(0, last, SPAN)]
    width = {g: end - g + (end == last) for g, end in groups}
    depth = [0] * slices
    for g, end in groups:
        for n in range(g, end + 1):
            depth[n] = width[g] - (n - g)
    deep = SPAN - 1
    inner = [0 if n in width and n else depth[n] for n in range(last + 1)]
    plan = []
    for g, end in groups:
        plan.append([(False, n, inner[n]) for n in range(g if g == 0 else g + 1, min(g + SPAN, last) + 1) if inner[n]])
    plan[0] += [(True, i, deep) for i in range(3)]
    packed = edges_packed(terms, factors, plan)

    def group_exchanged(g, state):
        group = plan[g // SPAN]
        far, near = packed[g // SPAN]
        pieces = [(factors if f else terms)[i] for f, i, _ in group]
        starts_at = offsets_of(group)
        if g:
            k = width[g]
            far = jnp.concatenate([jnp.where(even, state[:k], state[planes - k :]), far])
            near = jnp.concatenate([jnp.where(even, state[planes - k :], state[:k]), near])
            pieces, starts_at = [state] + pieces, [0] + [o + k for o in starts_at]
        far = lax.ppermute(far, "space", across_pairs())
        near = lax.ppermute(near, "space", beside_pairs())
        low, high = jnp.where(even, far, near), jnp.where(even, near, far)
        return [jnp.concatenate([low[o:e], x, high[o:e]]) for x, o, e in zip(pieces, starts_at, starts_at[1:])]

    def rows_exchanged(state):
        first_of_pair = place % 2 == 0
        top, bottom = state[:, HALO : 2 * HALO], state[:, part : part + HALO]
        within = swaps([(order[i], order[i + 1]) for i in range(0, slices - 1, 2)])
        between = swaps([(order[i], order[i + 1]) for i in range(1, slices - 1, 2)])
        inner_rows = lax.ppermute(jnp.where(first_of_pair, bottom, top), "tm", within)
        outer_rows = lax.ppermute(jnp.where(first_of_pair, top, bottom), "tm", between)
        above = jnp.where(first_of_pair, outer_rows, inner_rows)
        below = jnp.where(first_of_pair, inner_rows, outer_rows)
        return jnp.concatenate([above, state[:, HALO : HALO + part], below], axis=1)

    wide_terms = {n: terms[n] for n in range(slices)}
    sent = []
    state = terms[0]
    for n in range(last + 1):
        if n:
            k = inner[n]
            trim = deep - k
            o, s, w = (t[trim : t.shape[0] - trim] for t in coarse_terms)
            wide = state[depth[n - 1] - 1 - k : state.shape[0] - (depth[n - 1] - 1 - k)]
            total, upwind = around(wide)
            state = o * wide[1:-1] + s * total + w * upwind + wide_terms[n]
        if n in width:
            if n and n % HALO == 0:
                state = rows_exchanged(state)
            state, *more = group_exchanged(n, state)
            if n == 0:
                coarse_terms, more = more[-3:], more[:-3]
            for m, x in zip(range(n + 1, last + 1), more):
                wide_terms[m] = x
        k = depth[n]
        kept = state[:, HALO : HALO + part]
        sent.append(jnp.concatenate([kept[k : k + planes], jnp.where(even, kept[k - 1 : k], kept[k + planes : k + planes + 1])]))

    sent, element, slot, even, turned = lax.optimization_barrier((jnp.stack(sent[:1] + sent), element, slot, even, turned))
    back = lax.all_to_all(sent, "tm", 0, 0, tiled=True)
    back, element, slot, even, turned = lax.optimization_barrier((back, element, slot, even, turned))
    pairs = back.reshape((slices // 2, 2) + back.shape[1:])
    back = jnp.where(turned == 1, pairs[:, ::-1], pairs).reshape(back.shape)
    arrived = back.transpose(1, 0, 2, 3).reshape(planes + 1, rows, lanes)
    following, across = arrived[:planes], arrived[planes:]
    beside = lax.ppermute(jnp.where(even, following[planes - 1 :], following[:1]), "space", beside_pairs())
    low, high = jnp.where(even, across, beside), jnp.where(even, beside, across)
    coarse = coarse_linear(lax.optimization_barrier(jnp.concatenate([low, following, high])), raw[:3])
    end_state = jnp.where(slot > 0, coarse, 0.0) + element
    following = jnp.where(slot == 0, start, following)
    return end_state[None], following[None]


def solution(mesh):
    return jax.shard_map(
        on_device,
        mesh=mesh,
        in_specs=(
            P("tm", "space", None, None),
            P("space", None, None),
            P("space", None, None),
            P("space", None, None),
            P("space", None, None),
        ),
        out_specs=(P("tm", "space", None, None), P("tm", "space", None, None)),
        check_vma=False,
    )
```

```python
import jax
import jax.numpy as jnp
from jax import lax
from jax.experimental import pallas as pl
from jax.experimental.pallas import tpu as pltpu
from jax.sharding import PartitionSpec as P

FINE = 8
SPAN = 4
ROUNDS = 2
HALO = 8
OLD_TURN = 1


def swaps(pairs):
    return [route for a, b in pairs for route in ((a, b), (b, a))]


def beside_pairs():
    return swaps([(i, i + 1) for i in range(0, lax.axis_size("space") - 1, 2)])


def across_pairs():
    return swaps([(i, i + 1) for i in range(1, lax.axis_size("space") - 1, 2)])


def exchanged(low, high, even):
    across = lax.ppermute(jnp.where(even, low, high), "space", across_pairs())
    beside = lax.ppermute(jnp.where(even, high, low), "space", beside_pairs())
    return jnp.where(even, across, beside), jnp.where(even, beside, across)


def around(wide):
    padded = jnp.pad(wide, ((0, 0), (1, 1), (1, 1)))
    total = padded[2:, 1:-1, 1:-1] + padded[:-2, 1:-1, 1:-1]
    total = total + padded[1:-1, 2:, 1:-1] + padded[1:-1, :-2, 1:-1]
    total = total + padded[1:-1, 1:-1, 2:] + padded[1:-1, 1:-1, :-2]
    return total, wide[:-2]


def fine_step(wide, terms):
    d, c, l, h = terms
    total, upwind = around(wide)
    centre = wide[1:-1]
    return centre + d * (total - 6.0 * centre) - c * (centre - upwind) - l * centre + h


def coarse_linear(wide, terms):
    d, c, l = terms
    total, upwind = around(wide)
    return (wide[1:-1] + FINE * (d * total + c * upwind)) / (1.0 + FINE * (6.0 * d + c + l))


def edges_packed(terms, factors, plan):
    planes, rows, lanes = terms.shape[1:]
    pieces = [(g, o, k, f, i) for g, group in enumerate(plan) for o, (f, i, k) in zip(offsets_of(group), group)]

    def kernel(terms_ref, factors_ref, *refs):
        outs, sems = refs[:-1], refs[-1]
        odd = lax.axis_index("space") % 2
        copies = []
        for j, (g, o, k, f, i) in enumerate(pieces):
            source = (factors_ref if f else terms_ref).at[i]
            for side in range(2):
                at = (odd if side == 0 else 1 - odd) * (planes - k)
                copies.append(
                    pltpu.make_async_copy(source.at[pl.ds(at, k)], outs[2 * g + side].at[pl.ds(o, k)], sems.at[2 * j + side])
                )
        for copy in copies:
            copy.start()
        for copy in copies:
            copy.wait()

    sizes = [sum(k for _, _, k in group) for group in plan]
    shapes = [jax.ShapeDtypeStruct((n, rows, lanes), terms.dtype) for n in sizes for _ in range(2)]
    anywhere = pl.BlockSpec(memory_space=pl.ANY)
    outs = pl.pallas_call(
        kernel,
        name="edges_packed",
        out_shape=shapes,
        in_specs=[anywhere, anywhere],
        out_specs=[anywhere] * len(shapes),
        scratch_shapes=[pltpu.SemaphoreType.DMA((2 * len(pieces),))],
        compiler_params=pltpu.CompilerParams(vmem_limit_bytes=1 << 20),
    )(terms, factors)
    return [(outs[2 * g], outs[2 * g + 1]) for g in range(len(plan))]


def offsets_of(group):
    out = [0]
    for _, _, k in group:
        out.append(out[-1] + k)
    return out


def snake(index):
    turned = (index // 2) % 2
    return index + turned * (1 - 2 * (index % 2))


def on_device(slice_starts, diffusion, courant, loss, heating):
    start = slice_starts[0]
    planes, rows, lanes = start.shape
    slices = lax.axis_size("tm")
    slot = lax.axis_index("tm")
    even = lax.axis_index("space") % 2 == 0
    part = rows // slices
    window = part + 2 * HALO
    order = [snake(i) for i in range(slices)]
    raw = (diffusion, courant, loss, heating)

    def flat(*arrays):
        return jnp.concatenate([a.reshape(-1, lanes) for a in arrays])

    edge = ROUNDS - 1
    before, after = exchanged(flat(*(x[:edge] for x in raw)), flat(*(x[planes - edge :] for x in raw)), even)
    before, after = before.reshape(4, edge, rows, lanes), after.reshape(4, edge, rows, lanes)
    fine_terms = lax.optimization_barrier(jnp.concatenate([before, lax.optimization_barrier(jnp.stack(raw)), after], axis=1))
    raw = [x[edge : edge + planes] for x in fine_terms]

    state = start
    for turn in range(FINE // ROUNDS):
        low, high = state[:ROUNDS], state[planes - ROUNDS :]
        if turn == OLD_TURN:
            low, high, first = lax.optimization_barrier((low, high, first))
        low, high = exchanged(low, high, even)
        if turn == OLD_TURN:
            old = coarse_linear(first, raw[:3])
            low, high, old = lax.optimization_barrier((low, high, old))
        state = jnp.concatenate([low, state, high])
        if turn == 0:
            first = state[ROUNDS - 1 : ROUNDS + planes + 1]
        for step in range(ROUNDS):
            state = fine_step(state, [t[step : t.shape[0] - step] for t in fine_terms])
    element = jnp.where(slot > 0, state - old, state)

    place = snake(slot)
    line = place * part - HALO + lax.broadcasted_iota(jnp.int32, (1, window, 1), 1)
    inside = ((line >= 0) & (line < rows)).astype(jnp.float32)
    d, c, l = (
        lax.dynamic_slice_in_dim(jnp.pad(x, ((0, 0), (HALO, HALO), (0, 0))), place * part, window, axis=1) for x in raw[:3]
    )
    scale = inside / (1.0 + FINE * (6.0 * d + c + l))
    factors = jnp.stack([scale, FINE * d * scale, FINE * c * scale])

    tall = jnp.pad(element, ((0, 0), (HALO, HALO), (0, 0)))
    widened = jnp.stack([tall[:, p * part : p * part + window] for p in order])
    turned = lax.broadcasted_iota(jnp.int32, (slices // 2, 1, 1, 1, 1), 0) % 2
    kept = (element, factors, slot, even, place, turned)
    widened, *kept = lax.optimization_barrier((widened, *kept))
    terms = lax.all_to_all(widened, "tm", 0, 0, tiled=True)
    terms, element, factors, slot, even, place, turned = lax.optimization_barrier((terms, *kept))

    last = slices - 2
    groups = [(g, min(g + SPAN, last)) for g in range(0, last, SPAN)]
    width = {g: end - g + (end == last) for g, end in groups}
    depth = [0] * slices
    for g, end in groups:
        for n in range(g, end + 1):
            depth[n] = width[g] - (n - g)
    deep = SPAN - 1
    inner = [0 if n in width and n else depth[n] for n in range(last + 1)]
    plan = []
    for g, end in groups:
        plan.append([(False, n, inner[n]) for n in range(g if g == 0 else g + 1, min(g + SPAN, last) + 1) if inner[n]])
    plan[0] += [(True, i, deep) for i in range(3)]
    packed = edges_packed(terms, factors, plan)

    def group_exchanged(g, state):
        group = plan[g // SPAN]
        far, near = packed[g // SPAN]
        pieces = [(factors if f else terms)[i] for f, i, _ in group]
        starts_at = offsets_of(group)
        if g:
            k = width[g]
            far = jnp.concatenate([jnp.where(even, state[:k], state[planes - k :]), far])
            near = jnp.concatenate([jnp.where(even, state[planes - k :], state[:k]), near])
            pieces, starts_at = [state] + pieces, [0] + [o + k for o in starts_at]
        far = lax.ppermute(far, "space", across_pairs())
        near = lax.ppermute(near, "space", beside_pairs())
        low, high = jnp.where(even, far, near), jnp.where(even, near, far)
        return [jnp.concatenate([low[o:e], x, high[o:e]]) for x, o, e in zip(pieces, starts_at, starts_at[1:])]

    def rows_exchanged(state):
        first_of_pair = place % 2 == 0
        top, bottom = state[:, HALO : 2 * HALO], state[:, part : part + HALO]
        within = swaps([(order[i], order[i + 1]) for i in range(0, slices - 1, 2)])
        between = swaps([(order[i], order[i + 1]) for i in range(1, slices - 1, 2)])
        inner_rows = lax.ppermute(jnp.where(first_of_pair, bottom, top), "tm", within)
        outer_rows = lax.ppermute(jnp.where(first_of_pair, top, bottom), "tm", between)
        above = jnp.where(first_of_pair, outer_rows, inner_rows)
        below = jnp.where(first_of_pair, inner_rows, outer_rows)
        return jnp.concatenate([above, state[:, HALO : HALO + part], below], axis=1)

    wide_terms = {n: terms[n] for n in range(slices)}
    sent = []
    state = terms[0]
    for n in range(last + 1):
        if n:
            k = inner[n]
            trim = deep - k
            o, s, w = (t[trim : t.shape[0] - trim] for t in coarse_terms)
            wide = state[depth[n - 1] - 1 - k : state.shape[0] - (depth[n - 1] - 1 - k)]
            total, upwind = around(wide)
            state = o * wide[1:-1] + s * total + w * upwind + wide_terms[n]
        if n in width:
            if n and n % HALO == 0:
                state = rows_exchanged(state)
            state, *more = group_exchanged(n, state)
            if n == 0:
                coarse_terms, more = more[-3:], more[:-3]
            for m, x in zip(range(n + 1, last + 1), more):
                wide_terms[m] = x
        k = depth[n]
        kept = state[:, HALO : HALO + part]
        sent.append(jnp.concatenate([kept[k : k + planes], jnp.where(even, kept[k - 1 : k], kept[k + planes : k + planes + 1])]))

    sent, element, slot, even, turned = lax.optimization_barrier((jnp.stack(sent[:1] + sent), element, slot, even, turned))
    back = lax.all_to_all(sent, "tm", 0, 0, tiled=True)
    back, element, slot, even, turned = lax.optimization_barrier((back, element, slot, even, turned))
    pairs = back.reshape((slices // 2, 2) + back.shape[1:])
    back = jnp.where(turned == 1, pairs[:, ::-1], pairs).reshape(back.shape)
    arrived = back.transpose(1, 0, 2, 3).reshape(planes + 1, rows, lanes)
    following, across = arrived[:planes], arrived[planes:]
    beside = lax.ppermute(jnp.where(even, following[planes - 1 :], following[:1]), "space", beside_pairs())
    low, high = jnp.where(even, across, beside), jnp.where(even, beside, across)
    coarse = coarse_linear(lax.optimization_barrier(jnp.concatenate([low, following, high])), raw[:3])
    end_state = jnp.where(slot > 0, coarse, 0.0) + element
    following = jnp.where(slot == 0, start, following)
    return end_state[None], following[None]


def solution(mesh):
    return jax.shard_map(
        on_device,
        mesh=mesh,
        in_specs=(
            P("tm", "space", None, None),
            P("space", None, None),
            P("space", None, None),
            P("space", None, None),
            P("space", None, None),
        ),
        out_specs=(P("tm", "space", None, None), P("tm", "space", None, None)),
        check_vma=False,
    )
```
